128 devices in a mesh: tile: 64 (over z, x_lo, y, core), mem: 2 (over x_hi).
Axes of the slice: x: 4 (x_hi: 2, x_lo: 2; x = x_hi * 2 + x_lo), y: 4, z: 4, core: 2. Of those that a mesh axis runs over, the one named last changes fastest.
Arguments:
- control: bfloat16 [4, 64, 768, 1536], P('mem', None, 'tile'), may hold values from -6 to 6
- members: bfloat16 [4, 64, 768, 1536], P('mem', None, 'tile'), may hold values from -6 to 6
- gradient: bfloat16 [64, 768, 1536], P('tile'), may hold values from -6 to 6
- step_x: float32 [1536], replicated, may hold values from 0.1 to 0.4
- step_y: float32 [768], replicated, may hold values from 0.01 to 0.1
- step_z: float32 [64], replicated, may hold values from 0.1 to 1
Outputs:
- increment: bfloat16 [64, 768, 1536], P('tile')
- control_grad: bfloat16 [4, 64, 768, 1536], P('mem', None, 'tile')
The draws below stay inside these ranges and needn't reach their ends.
All inputs are finite; a program needn't handle non-finite values.
Results may differ from the reference program's by a relative error of at most 0.0085.
Values may be sent and summed in bfloat16 or wider, within the bound.
A program may use at most 128 MiB of HBM per device.

```python
import math
import jax
import jax.numpy as jnp
from jax import lax

NX = 1536
NY = 768
NZ = 64
MEMBERS = 4
BAND = 8


def shard_levels(rng, dims, split, least, high):
    factor_of = 1.0
    for axis_at, shards_of in split:
        steps = jax.random.uniform(jax.random.fold_in(jax.random.fold_in(rng, 6), axis_at), (shards_of,), jnp.float32, least / len(split), high / len(split))
        factor_of = factor_of * jnp.repeat(jnp.exp(steps), dims[axis_at] // shards_of).reshape((-1,) + (1,) * (len(dims) - 1 - axis_at))
    return factor_of


def centred(rng, shape, width, bound, shards=(), kind=jnp.bfloat16):
    level = shard_levels(rng, shape, shards, -0.22, 0.18) if shards else 1.0
    array = jax.random.normal(rng, shape, jnp.float32) * width * level
    return jnp.minimum(jnp.maximum(array, -bound), bound).astype(kind)


def setup_inputs(seed: int = 0) -> dict:
    streams_of = jax.random.split(jax.random.key(seed), 7)
    return {
        "control": centred(streams_of[0], (MEMBERS, NZ, NY, NX), 1.0, 6.0, ((0, 2), (2, 64))),
        "members": centred(streams_of[1], (MEMBERS, NZ, NY, NX), 1.0, 6.0, ((0, 2), (2, 64))),
        "gradient": centred(streams_of[2], (NZ, NY, NX), 1.0, 6.0, ((0, 64),)),
        "step_x": jnp.clip(jnp.exp(jax.random.uniform(streams_of[3], (NX,), jnp.float32, math.log(0.1), math.log(0.4))), 0.1, 0.4),
        "step_y": jnp.clip(jnp.exp(jax.random.uniform(streams_of[4], (NY,), jnp.float32, math.log(0.01), math.log(0.1))), 0.01, 0.1),
        "step_z": jnp.clip(jnp.exp(jax.random.uniform(streams_of[5], (NZ,), jnp.float32, math.log(0.1), math.log(1.0))), 0.1, 1.0),
    }


along_gain = 0.35
horiz_gain = 0.15
vert_gain = 0.5


def kernel_matrix(steps, gain):
    coord = jnp.cumsum(steps.astype(jnp.float32))
    return gain * jnp.exp(-jnp.abs(coord[:, None] - coord[None, :]))


def build_filters(step_x, step_y, step_z):
    filter_x = kernel_matrix(step_x, along_gain).astype(jnp.bfloat16)
    filter_y = kernel_matrix(step_y, horiz_gain).astype(jnp.bfloat16)
    level_ids = jnp.arange(step_z.shape[0], dtype=jnp.int32)
    banded = jnp.abs(level_ids[:, None] - level_ids[None, :]) <= BAND
    filter_z = jnp.where(banded, kernel_matrix(step_z, vert_gain), jnp.float32(0.0)).astype(jnp.bfloat16)
    return filter_x, filter_y, filter_z


def along_y(filter_y, field):
    return lax.map(lambda level: jnp.dot(filter_y, level, preferred_element_type=jnp.float32).astype(jnp.bfloat16), field)


def reference(control, members, gradient, step_x, step_y, step_z):
    filter_x, filter_y, filter_z = build_filters(step_x, step_y, step_z)
    grad_wide = gradient.astype(jnp.float32)

    def one_member(carry, pair):
        ctrl, memb = pair
        vert = jnp.dot(filter_z, ctrl.reshape(NZ, NY * NX), preferred_element_type=jnp.float32).astype(jnp.bfloat16)
        along = jnp.dot(vert.reshape(NZ * NY, NX), filter_x, preferred_element_type=jnp.float32).astype(jnp.bfloat16)
        shaped = along_y(filter_y, along.reshape(NZ, NY, NX))
        carry = carry + memb.astype(jnp.float32) * shaped.astype(jnp.float32)
        weighted = (memb.astype(jnp.float32) * grad_wide).astype(jnp.bfloat16)
        adj_y = along_y(filter_y, weighted)
        adj_x = jnp.dot(adj_y.reshape(NZ * NY, NX), filter_x, preferred_element_type=jnp.float32).astype(jnp.bfloat16)
        result = jnp.dot(filter_z.T, adj_x.reshape(NZ, NY * NX), preferred_element_type=jnp.float32).astype(jnp.bfloat16)
        return carry, result.reshape(NZ, NY, NX)

    total, grads = lax.scan(one_member, jnp.zeros((NZ, NY, NX), jnp.float32), (control, members))
    return total.astype(jnp.bfloat16), grads
```

```python
import jax
import jax.numpy as jnp
from jax import lax
from jax.sharding import PartitionSpec as P

BAND = 8

along_gain = 0.35
horiz_gain = 0.15
vert_gain = 0.5
BF = jnp.bfloat16
F32 = jnp.float32


def kernel_matrix(coord, gain):
    return gain * jnp.exp(-jnp.abs(coord[:, None] - coord[None, :]))


def chip_of(tile, mem):
    z, x_lo, y, core = tile // 16, tile // 8 % 2, tile // 2 % 4, tile % 2
    return z, mem * 2 + x_lo, y, core


def x_shift(by):
    pairs = []
    for tile in range(64):
        for mem in range(2):
            z, x, y, core = chip_of(tile, mem)
            nx = (x + by) % 4
            pairs.append((tile * 2 + mem, (z * 16 + nx % 2 * 8 + y * 2 + core) * 2 + nx // 2))
    return pairs


def body(control, members, gradient, step_x, step_y, step_z):
    t = lax.axis_index("tile")
    x_hi = lax.axis_index("mem")
    x_lo = t // 8 % 2
    nx = step_x.shape[0]
    nz = step_z.shape[0]
    blocks = 64
    rows = step_y.shape[0] // blocks

    filter_x = kernel_matrix(jnp.cumsum(step_x), along_gain).astype(BF)
    ids = jnp.arange(nz, dtype=jnp.int32)
    banded = jnp.abs(ids[:, None] - ids[None, :]) <= BAND
    filter_z = jnp.where(banded, kernel_matrix(jnp.cumsum(step_z), vert_gain), 0.0).astype(BF)

    coord = jnp.cumsum(step_y).reshape(blocks, rows)
    here = lax.dynamic_index_in_dim(coord, t, 0, keepdims=False)
    first, last = coord[:, 0], coord[:, -1]
    local = kernel_matrix(here, horiz_gain).astype(BF).astype(F32)
    take_low = jnp.exp(here - here[-1])
    take_high = jnp.exp(here[0] - here)
    give_low = horiz_gain * take_high
    give_high = horiz_gain * take_low
    mix = jnp.concatenate([local, take_low[None], take_high[None]], 0)
    order = jnp.arange(blocks)
    below = order[None, :] < order[:, None]
    from_low = jnp.where(below, jnp.exp(jnp.minimum(last[None, :] - first[:, None], 0.0)), 0.0)
    from_high = jnp.where(below.T, jnp.exp(jnp.minimum(last[:, None] - first[None, :], 0.0)), 0.0)
    spread = jnp.stack([from_low, from_high]).astype(BF)

    def kron(fz):
        return (mix[:, None, :, None] * fz.astype(F32)[None, :, None, :]).astype(BF).reshape((rows + 2) * nz, rows * nz)

    def filtered(fields, fz):
        mixed = jnp.einsum(
            "ab,mbx->max", kron(fz), fields.reshape(2, rows * nz, nx), preferred_element_type=F32
        ).astype(BF).reshape(2, rows + 2, nz, nx)
        carry = mixed[:, rows:].transpose(2, 0, 1, 3)
        got = lax.all_to_all(carry, "tile", split_axis=0, concat_axis=0, tiled=True)
        sums = jnp.einsum("rde,emrx->dmrx", spread, got, preferred_element_type=F32).astype(BF)
        back = lax.all_to_all(sums, "tile", split_axis=0, concat_axis=0, tiled=True)
        base = jnp.einsum("myzk,kx->myzx", mixed[:, :rows], filter_x, preferred_element_type=F32).astype(BF)
        edge = jnp.einsum("zmrk,kx->mrzx", back, filter_x, preferred_element_type=F32).astype(BF)
        edge = edge.astype(F32)
        return (
            base.astype(F32)
            + give_low[None, :, None, None] * edge[:, 0][:, None]
            + give_high[None, :, None, None] * edge[:, 1][:, None]
        )

    fields = control.transpose(0, 2, 1, 3)
    weights = members.transpose(0, 2, 1, 3).astype(F32)

    grad_rows = lax.all_to_all(gradient.reshape(blocks, rows, nx), "tile", split_axis=0, concat_axis=0, tiled=True)
    shaped = filtered(fields, filter_z)
    partial = jnp.sum(weights * shaped, axis=0).astype(BF).transpose(1, 0, 2)
    weighted = (weights * grad_rows.transpose(1, 0, 2).astype(F32)[None]).astype(BF)

    split = partial.reshape(4, 2, 8, rows, nx)
    own = lax.dynamic_index_in_dim(split, x_lo, 1, keepdims=False)
    other = lax.dynamic_index_in_dim(split, 1 - x_lo, 1, keepdims=False)
    near, far = own[:2], own[2:]
    is_low = x_hi == 0
    up = jnp.concatenate([other, jnp.where(is_low, near, far)], 0)
    down = jnp.concatenate([other, jnp.where(is_low, far, near)], 0)
    axes = ("tile", "mem")
    a = lax.ppermute(up, axes, x_shift(1)).astype(F32)
    b = lax.ppermute(down, axes, x_shift(-1)).astype(F32)
    both = (a + b).astype(BF)
    neighbour_rows, relay = both[:4], both[4:]
    c = lax.ppermute(relay, axes, x_shift(1))
    d = lax.ppermute(relay, axes, x_shift(-1))
    own_rows = jnp.concatenate([jnp.where(is_low, d, c), jnp.where(is_low, c, d)], 0)
    flip = x_lo == 0
    lanes = jnp.stack([jnp.where(flip, own_rows, neighbour_rows), jnp.where(flip, neighbour_rows, own_rows)], 2)
    groups = [[z * 16 + xl * 8 + k for z in range(4) for k in range(8)] for xl in range(2)]
    level = lax.all_to_all(
        lanes.reshape(32, 2, rows, nx), "tile", split_axis=0, concat_axis=0, axis_index_groups=groups, tiled=True
    )
    increment = level.reshape(4, 8, 2, rows, nx).transpose(0, 2, 1, 3, 4).reshape(1, blocks * rows, nx)

    control_grad = filtered(weighted, filter_z.T).astype(BF).transpose(0, 2, 1, 3)
    return (increment, control_grad)


def solution(mesh):
    placed = (
        P("mem", None, "tile", None),
        P("mem", None, "tile", None),
        P("tile", None, None),
        P(),
        P(),
        P(),
    )
    return jax.shard_map(
        body,
        mesh=mesh,
        in_specs=placed,
        out_specs=(P("tile", None, None), P("mem", None, "tile", None)),
        check_vma=False,
    )
```

```python
import functools

import jax
import jax.numpy as jnp
from jax import lax
from jax.experimental import pallas as pl
from jax.experimental.pallas import tpu as pltpu
from jax.sharding import PartitionSpec as P

BAND = 8

along_gain = 0.35
horiz_gain = 0.15
vert_gain = 0.5
BF = jnp.bfloat16
F32 = jnp.float32
MESH = pl.DeviceIdType.MESH

NX = 1536
NZ = 64
ROWS = 12
CHIPS = 32
XB = 256
NB = NX // XB
SZ = 16
SX = 384
EY, UY, VY, KC, G1, G2, SA, SB = 0, 16, 32, 48, 49, 50, 64, 96


def kernel_matrix(coord, gain):
    return gain * jnp.exp(-jnp.abs(coord[:, None] - coord[None, :]))


def decay(gap):
    return jnp.exp(-jnp.maximum(gap, 0.0))


def chip_of(tile, mem):
    z, x_lo, y, core = tile // 16, tile // 8 % 2, tile // 2 % 4, tile % 2
    return z, mem * 2 + x_lo, y, core


def x_shift(by):
    pairs = []
    for tile in range(64):
        for mem in range(2):
            z, x, y, core = chip_of(tile, mem)
            nx = (x + by) % 4
            pairs.append((tile * 2 + mem, (z * 16 + nx % 2 * 8 + y * 2 + core) * 2 + nx // 2))
    return pairs


def filter_kernel(
    adjoint, coef, field_hbm, memb_hbm, fz, fb, wc, ux, out_hbm,
    field, memb, local, inner, vz, fore, ends, pin, comb, gath, res, chipc, edges, wide,
    in_sem, out_sem, pair_sem, send1, recv1, send2, recv2,
):
    t = lax.axis_index("tile")
    mem = lax.axis_index("mem")
    c = t % 2
    me = t // 2
    half = ROWS * NZ

    field_loads = []
    memb_loads = [pltpu.make_async_copy(memb_hbm.at[m], memb.at[m], in_sem.at[2 + m]) for m in range(2)]
    for m in range(1 if adjoint else 2):
        field_loads.append(pltpu.make_async_copy(field_hbm.at[m], field.at[m], in_sem.at[m]))
        field_loads[m].start()
    for load in memb_loads:
        load.start()

    barrier = pltpu.get_barrier_semaphore()
    partner = (me * 2 + 1 - c, mem)
    pl.semaphore_signal(barrier, inc=1, device_id=partner, device_id_type=MESH)

    def greet(k, _):
        j = (me + k) % CHIPS
        pl.semaphore_signal(barrier, inc=1, device_id=(j * 2 + c, mem), device_id_type=MESH)
        return 0

    lax.fori_loop(1, CHIPS, greet, 0)

    def span(y, n=1):
        return pl.ds(NZ * y, NZ * n)

    for m in range(2):
        if adjoint:
            if m == 0:
                field_loads[0].wait()
            memb_loads[m].wait()
        else:
            field_loads[m].wait()

        def columns(n, _):
            cols = pl.ds(pl.multiple_of(n * XB, XB), XB)
            for g in range(3):
                rows = span(4 * g, 4)
                if adjoint:
                    tile = (memb[m, rows, cols].astype(F32) * field[0, rows, cols].astype(F32)).astype(BF)
                else:
                    tile = field[m, rows, cols]
                vz[rows] = jnp.dot(fz[...], tile, preferred_element_type=F32)
            p = vz[span(0)]
            fore[span(0)] = p
            for y in range(1, ROWS):
                p = vz[span(y)] + coef[EY + y] * p
                fore[span(y)] = p
            ends[0, m, :, cols] = p.astype(BF)
            q = vz[span(ROWS - 1)]
            local[m, span(ROWS - 1), cols] = (horiz_gain * p).astype(BF)
            for y in range(ROWS - 2, -1, -1):
                back = coef[EY + y + 1] * q
                local[m, span(y), cols] = (horiz_gain * (fore[span(y)] + back)).astype(BF)
                q = vz[span(y)] + back
            ends[1, m, :, cols] = q.astype(BF)
            return 0

        lax.fori_loop(0, NB, columns, 0)

    pl.semaphore_wait(barrier, CHIPS)
    swap = pltpu.make_async_remote_copy(
        src_ref=ends.at[c], dst_ref=pin, send_sem=pair_sem.at[0], recv_sem=pair_sem.at[1],
        device_id=partner, device_id_type=MESH,
    )
    swap.start()
    swap.wait()
    for m in range(2):
        comb[m] = (ends[1 - c, m].astype(F32) + coef[KC] * pin[m].astype(F32)).astype(BF)

    def piece(j):
        return j // 16, pl.ds(pl.multiple_of(j // 4 % 4 * SZ, SZ), SZ), pl.ds(pl.multiple_of(j % 4 * SX, 128), SX)

    mine = piece(me)

    def scatter(j, slot):
        return pltpu.make_async_remote_copy(
            src_ref=comb.at[piece(j)], dst_ref=gath.at[slot], send_sem=send1.at[j], recv_sem=recv1.at[slot],
            device_id=(j * 2 + c, mem), device_id_type=MESH,
        )

    def gather(j, slot):
        return pltpu.make_async_remote_copy(
            src_ref=res.at[j], dst_ref=chipc.at[piece(slot)], send_sem=send2.at[j], recv_sem=recv2.at[slot],
            device_id=(j * 2 + c, mem), device_id_type=MESH,
        )

    def every(do):
        def step(k, _):
            do((me + k) % CHIPS)
            return 0

        lax.fori_loop(1, CHIPS, step, 0)

    def x_filter(src, store):
        rows = src.shape[0]
        inner[pl.ds(0, rows)] = jnp.dot(src[...], wc[...], preferred_element_type=F32).astype(BF)

        def block(b, _):
            cols = pl.ds(pl.multiple_of(b * XB, XB), XB)
            store(
                cols,
                jnp.dot(src[:, cols], fb[b], preferred_element_type=F32)
                + jnp.dot(inner[pl.ds(0, rows)], ux[:, cols], preferred_element_type=F32),
            )
            return 0

        lax.fori_loop(0, NB, block, 0)

    def base(m):
        def keep(cols, value):
            local[m, :, cols] = value.astype(BF)

        x_filter(local.at[m], keep)

    every(lambda j: scatter(j, me).start())
    gath[me] = comb[mine]
    base(0)

    def end_scatter(j):
        scatter(j, j).wait_recv()
        scatter(j, me).wait_send()

    every(end_scatter)

    def scan(i, run):
        d = c * i + (1 - c) * (CHIPS - 1 - i)
        res[d] = run.astype(BF)
        return coef[SA + i] * gath[d].astype(F32) + coef[SB + i] * run

    lax.fori_loop(0, CHIPS, scan, jnp.zeros((SZ, SX), F32))
    every(lambda j: gather(j, me).start())
    chipc[mine] = res[me]
    base(1)

    def end_gather(j):
        gather(j, j).wait_recv()
        gather(j, me).wait_send()

    every(end_gather)

    def hand_over(slot):
        return pltpu.make_async_remote_copy(
            src_ref=chipc, dst_ref=edges.at[slot], send_sem=pair_sem.at[2], recv_sem=pair_sem.at[3],
            device_id=partner, device_id_type=MESH,
        )

    hand_over(1 - c).start()
    for m in range(2):
        edges[1 - c, m] = (coef[G1] * pin[m].astype(F32) + coef[G2] * chipc[m].astype(F32)).astype(BF)
    hand_over(c).wait_recv()
    hand_over(1 - c).wait_send()

    for r in range(2):
        for m in range(2):
            comb[m] = edges[r, m]

        for m in range(2):
            def keep_edge(cols, value):
                wide[r, m, :, cols] = value

            x_filter(comb.at[m], keep_edge)

    if not adjoint:
        for load in memb_loads:
            load.wait()

    def blend(n, _):
        cols = pl.ds(pl.multiple_of(n * 128, 128), 128)
        for y in range(ROWS):
            total = None
            for m in range(2):
                value = (
                    local[m, span(y), cols].astype(F32)
                    + coef[UY + y] * wide[0, m, :, cols]
                    + coef[VY + y] * wide[1, m, :, cols]
                )
                if adjoint:
                    local[m, span(y), cols] = value.astype(BF)
                else:
                    value = value * memb[m, span(y), cols].astype(F32)
                    total = value if m == 0 else total + value
            if not adjoint:
                local[0, span(y), cols] = total.astype(BF)
        return 0

    lax.fori_loop(0, NX // 128, blend, 0)
    stores = [
        pltpu.make_async_copy(local.at[m], out_hbm.at[m], out_sem.at[m]) for m in range(2 if adjoint else 1)
    ]
    for s in stores:
        s.start()
    for s in stores:
        s.wait()


def filter_call(adjoint, coef, field, memb, fz, fb, wc, ux):
    any_space = pl.BlockSpec(memory_space=pl.ANY)
    vmem = pl.BlockSpec(memory_space=pltpu.VMEM)
    half = ROWS * NZ
    n = 2 if adjoint else 1
    dma = pltpu.SemaphoreType.DMA
    return pl.pallas_call(
        functools.partial(filter_kernel, adjoint),
        out_shape=jax.ShapeDtypeStruct((n, half, NX), BF),
        in_specs=[pl.BlockSpec(memory_space=pltpu.SMEM), any_space, any_space, vmem, vmem, vmem, vmem],
        out_specs=any_space,
        scratch_shapes=[
            pltpu.VMEM((3 - n, half, NX), BF),
            pltpu.VMEM((2, half, NX), BF),
            pltpu.VMEM((2, half, NX), BF),
            pltpu.VMEM((half, 128), BF),
            pltpu.VMEM((half, XB), F32),
            pltpu.VMEM((half, XB), F32),
            pltpu.VMEM((2, 2, NZ, NX), BF),
            pltpu.VMEM((2, NZ, NX), BF),
            pltpu.VMEM((2, NZ, NX), BF),
            pltpu.VMEM((CHIPS, SZ, SX), BF),
            pltpu.VMEM((CHIPS, SZ, SX), BF),
            pltpu.VMEM((2, NZ, NX), BF),
            pltpu.VMEM((2, 2, NZ, NX), BF),
            pltpu.VMEM((2, 2, NZ, NX), F32),
            dma((4,)),
            dma((2,)),
            dma((4,)),
            dma((CHIPS,)),
            dma((CHIPS,)),
            dma((CHIPS,)),
            dma((CHIPS,)),
        ],
        compiler_params=pltpu.CompilerParams(
            collective_id=n, has_side_effects=True, vmem_limit_bytes=40 * 1024 * 1024
        ),
        cost_estimate=pl.CostEstimate(flops=10_000_000_000, bytes_accessed=14_000_000, transcendentals=0),
        name="adjoint_filter" if adjoint else "forward_filter",
    )(coef, field, memb, fz, fb, wc, ux)


def tables(step_x, step_y, step_z, t):
    cx = jnp.cumsum(step_x)
    blocks = cx.reshape(NB, XB)
    fb = (along_gain * jnp.exp(-jnp.abs(blocks[:, :, None] - blocks[:, None, :]))).astype(BF)
    low, high = blocks[:, 0], blocks[:, -1]
    owner = jnp.arange(NX)[:, None] // XB
    ids = jnp.arange(NB)[None, :]
    from_low = jnp.where(owner < ids, decay(low[None, :] - cx[:, None]), 0.0)
    from_high = jnp.where(owner > ids, decay(cx[:, None] - high[None, :]), 0.0)
    fill = jnp.zeros((NX, 64 - NB), F32)
    wc = jnp.concatenate([from_low, fill, from_high, fill], 1).astype(BF)
    to_low = jnp.where(owner == ids, along_gain * decay(cx[:, None] - low[None, :]), 0.0)
    to_high = jnp.where(owner == ids, along_gain * decay(high[None, :] - cx[:, None]), 0.0)
    ux = jnp.concatenate([to_low, fill, to_high, fill], 1).T.astype(BF)

    ids = jnp.arange(NZ, dtype=jnp.int32)
    banded = jnp.abs(ids[:, None] - ids[None, :]) <= BAND
    fz = jnp.where(banded, kernel_matrix(jnp.cumsum(step_z), vert_gain), 0.0)
    eye = jnp.eye(4, dtype=F32)
    fz_up, fz_down = (
        (eye[:, None, :, None] * f[None, :, None, :]).reshape(4 * NZ, 4 * NZ).astype(BF) for f in (fz, fz.T)
    )

    c, me = t % 2, t // 2
    cy = jnp.cumsum(step_y)
    here = lax.dynamic_index_in_dim(cy.reshape(2 * CHIPS, ROWS), t, 0, keepdims=False)
    chips = cy.reshape(CHIPS, 2 * ROWS)
    chip = lax.dynamic_index_in_dim(chips, me, 0, keepdims=False)
    f0, l0, f1, l1 = chip[0], chip[ROWS - 1], chip[ROWS], chip[-1]
    first, last = chips[:, 0], chips[:, -1]
    following = jnp.concatenate([first[1:], first[-1:]])
    previous = jnp.concatenate([last[:1], last[:-1]])
    upper = c == 1
    ey = jnp.concatenate([jnp.zeros((1,), F32), decay(here[1:] - here[:-1])])
    pad = jnp.zeros((4,), F32)
    by_core = [
        jnp.where(upper, decay(l1 - l0), decay(f1 - f0)),
        decay(f1 - l0),
        jnp.where(upper, decay(f1 - f0), decay(l1 - l0)),
    ]
    sa = jnp.where(upper, decay(following - last), decay(first - previous)[::-1])
    sb = jnp.where(upper, decay(following - first), decay(last - previous)[::-1])
    coef = jnp.concatenate(
        [
            ey, pad,
            horiz_gain * decay(here - here[0]), pad,
            horiz_gain * decay(here[-1] - here), pad,
            jnp.stack(by_core), jnp.zeros((13,), F32),
            sa, sb,
        ]
    )
    return coef, fb, wc, ux, fz_up, fz_down


def body(control, members, gradient, step_x, step_y, step_z):
    t = lax.axis_index("tile")
    x_hi = lax.axis_index("mem")
    x_lo = t // 8 % 2
    blocks = 2 * CHIPS
    half = ROWS * NZ
    coef, fb, wc, ux, fz_up, fz_down = tables(step_x, step_y, step_z, t)

    grad_rows = lax.all_to_all(gradient.reshape(blocks, ROWS, NX), "tile", split_axis=0, concat_axis=0, tiled=True)
    grad_field = grad_rows.transpose(1, 0, 2).reshape(1, half, NX)
    fields = control.transpose(0, 2, 1, 3).reshape(2, half, NX)
    memb = members.transpose(0, 2, 1, 3).reshape(2, half, NX)

    partial = filter_call(False, coef, fields, memb, fz_up, fb, wc, ux)
    partial = partial.reshape(ROWS, NZ, NX).transpose(1, 0, 2)

    split = partial.reshape(4, 2, 8, ROWS, NX)
    own = lax.dynamic_index_in_dim(split, x_lo, 1, keepdims=False)
    other = lax.dynamic_index_in_dim(split, 1 - x_lo, 1, keepdims=False)
    near, far = own[:2], own[2:]
    is_low = x_hi == 0
    up = jnp.concatenate([other, jnp.where(is_low, near, far)], 0)
    down = jnp.concatenate([other, jnp.where(is_low, far, near)], 0)
    axes = ("tile", "mem")
    a = lax.ppermute(up, axes, x_shift(1)).astype(F32)
    b = lax.ppermute(down, axes, x_shift(-1)).astype(F32)
    both = (a + b).astype(BF)
    neighbour_rows, relay = both[:4], both[4:]
    down_back = lax.ppermute(relay, axes, x_shift(1))
    up_back = lax.ppermute(relay, axes, x_shift(-1))
    own_rows = jnp.concatenate(
        [jnp.where(is_low, up_back, down_back), jnp.where(is_low, down_back, up_back)], 0
    )
    flip = x_lo == 0
    lanes = jnp.stack([jnp.where(flip, own_rows, neighbour_rows), jnp.where(flip, neighbour_rows, own_rows)], 2)
    groups = [[z * 16 + xl * 8 + k for z in range(4) for k in range(8)] for xl in range(2)]
    level = lax.all_to_all(
        lanes.reshape(32, 2, ROWS, NX), "tile", split_axis=0, concat_axis=0, axis_index_groups=groups, tiled=True
    )
    increment = level.reshape(4, 8, 2, ROWS, NX).transpose(0, 2, 1, 3, 4).reshape(1, blocks * ROWS, NX)

    grads = filter_call(True, coef, grad_field, memb, fz_down, fb, wc, ux)
    control_grad = grads.reshape(2, ROWS, NZ, NX).transpose(0, 2, 1, 3)
    return (increment, control_grad)


def solution(mesh):
    placed = (
        P("mem", None, "tile", None),
        P("mem", None, "tile", None),
        P("tile", None, None),
        P(),
        P(),
        P(),
    )
    return jax.shard_map(
        body,
        mesh=mesh,
        in_specs=placed,
        out_specs=(P("tile", None, None), P("mem", None, "tile", None)),
        check_vma=False,
    )
```
